128 devices in a mesh: row: 4 (over y), col: 32 (over z, x, core).
Axes of the slice: x: 4, y: 4, z: 4, core: 2. Of those that a mesh axis runs over, the one named last changes fastest.
Arguments:
- tokens: bfloat16 [768, 8192], P('col', 'row'), may hold values from -6 to 6
- gate_weight: bfloat16 [8192, 28672], P('row', 'col'), may hold values from -0.0625 to 0.0625
- up_weight: bfloat16 [8192, 28672], P('row', 'col'), may hold values from -0.0625 to 0.0625
- down_weight: bfloat16 [28672, 8192], P('col', 'row'), may hold values from -0.03125 to 0.03125
- mask_gate: int32 [128, 448], P('row', 'col'), may hold values from 0 to 1, as said below
- mask_up: int32 [128, 448], P('row', 'col'), may hold values from 0 to 1, as said below
- mask_down: int32 [448, 128], P('col', 'row'), may hold values from 0 to 1, as said below
- cotangent: bfloat16 [768, 8192], P('col', 'row'), may hold values from -1.5 to 1.5
Outputs:
- output: bfloat16 [768, 8192], P('col', 'row')
- grad_input: bfloat16 [768, 8192], P('col', 'row')
- grad_gate: bfloat16 [8192, 28672], P('row', 'col')
- grad_up: bfloat16 [8192, 28672], P('row', 'col')
- grad_down: bfloat16 [28672, 8192], P('col', 'row')
The draws below stay inside these ranges and needn't reach their ends.
Inputs may be any that keep to these rules, and one draw needn't show every extreme that they name: `mask_gate`: 1 where a 64 x 64 block of the weight is kept, 0 where it is pruned. `mask_up`: 1 where a 64 x 64 block of the weight is kept, 0 where it is pruned. `mask_down`: 1 where a 64 x 64 block of the weight is kept, 0 where it is pruned.
All inputs are finite; a program needn't handle non-finite values.
Results may differ from the reference program's by a relative error of at most 0.006.
Values may be sent and summed in bfloat16 or wider, within the bound.
No kernel may reach another device: no remote copies, remote signals or barrier semaphores. Data moves between devices by JAX's collectives and lax.ppermute only.
A program may use at most 128 MiB of HBM per device.

```python
import jax
import jax.numpy as jnp
from jax import lax

D = 8192
FF = 28672
BLOCK = 64
TOKENS = 768
DB = 128
FB = 448
N_COL = 32


def column_mask(key, salt, rows, cols, group_axis):
    base = jax.random.fold_in(key, salt)
    dens_key = jax.random.fold_in(base, 1)
    cell_key = jax.random.fold_in(base, 2)
    density = jax.random.randint(dens_key, (N_COL,), 3, 10)
    cells = jax.random.randint(cell_key, (rows, cols), 0, 10)
    if group_axis == 1:
        groups = jnp.arange(cols, dtype=jnp.int32) // (cols // N_COL)
        level = density[groups][None, :]
    else:
        groups = jnp.arange(rows, dtype=jnp.int32) // (rows // N_COL)
        level = density[groups][:, None]
    return (cells < level).astype(jnp.int32)


def draw_mask_gate(key, part):
    return column_mask(key, 11, DB, FB, 1)


def draw_mask_up(key, part):
    return column_mask(key, 23, DB, FB, 1)


def draw_mask_down(key, part):
    return column_mask(key, 37, FB, DB, 0)


def levels(stream_key, extent, pieces, low, high):
    def one(dim, parts):
        draws = jax.random.uniform(jax.random.fold_in(jax.random.fold_in(stream_key, 6), dim), (parts,), jnp.float32, low / len(pieces), high / len(pieces))
        return jnp.repeat(jnp.exp(draws), extent[dim] // parts).reshape((-1,) + (1,) * (len(extent) - dim - 1))

    level = one(*pieces[0])
    for cut in pieces[1:]:
        level = level * one(*cut)
    return level


def normal_values(rng, extent, spread, bound, pieces=(), held_as=jnp.bfloat16):
    factor_of = levels(rng, extent, pieces, -0.22, 0.18) if pieces else 1.0
    array = jax.random.normal(rng, extent, jnp.float32) * spread * factor_of
    return jnp.minimum(jnp.maximum(array, -bound), bound).astype(held_as)


def setup_inputs(seed: int = 0) -> dict:
    seeds = jax.random.split(jax.random.key(seed), 9)
    tokens = normal_values(seeds[0], (TOKENS, D), 1.0, 6.0, ((0, 32), (1, 4)))
    gate_weight = normal_values(seeds[1], (D, FF), D ** -0.5, 0.0625, ((0, 4), (1, 32)))
    up_weight = normal_values(seeds[2], (D, FF), D ** -0.5, 0.0625, ((0, 4), (1, 32)))
    down_weight = normal_values(seeds[3], (FF, D), FF ** -0.5, 0.03125, ((0, 32), (1, 4)))
    mask_gate = draw_mask_gate(jax.random.fold_in(seeds[8], 71), 0)
    mask_up = draw_mask_up(jax.random.fold_in(seeds[8], 71), 0)
    mask_down = draw_mask_down(jax.random.fold_in(seeds[8], 71), 0)
    cotangent = normal_values(seeds[7], (TOKENS, D), 0.25, 1.5, ((0, 32), (1, 4)))
    return dict(tokens=tokens, gate_weight=gate_weight, up_weight=up_weight, down_weight=down_weight, mask_gate=mask_gate, mask_up=mask_up, mask_down=mask_down, cotangent=cotangent)


def expand(mask):
    return jnp.repeat(jnp.repeat(mask, BLOCK, 0), BLOCK, 1).astype(jnp.bfloat16)


def reference(tokens, gate_weight, up_weight, down_weight, mask_gate, mask_up, mask_down, cotangent):
    keep_gate = expand(mask_gate)
    keep_up = expand(mask_up)
    keep_down = expand(mask_down)
    w_gate = gate_weight * keep_gate
    w_up = up_weight * keep_up
    w_down = down_weight * keep_down
    gate = jnp.dot(tokens, w_gate, preferred_element_type=jnp.float32)
    up = jnp.dot(tokens, w_up, preferred_element_type=jnp.float32)
    sigma = jax.nn.sigmoid(gate)
    hidden = (gate * sigma * up).astype(jnp.bfloat16)
    output = jnp.dot(hidden, w_down, preferred_element_type=jnp.float32).astype(jnp.bfloat16)
    dhid = lax.dot_general(cotangent, w_down, (((1,), (1,)), ((), ())), preferred_element_type=jnp.float32)
    dgate = (dhid * up * sigma * (1.0 + gate * (1.0 - sigma))).astype(jnp.bfloat16)
    dup = (dhid * gate * sigma).astype(jnp.bfloat16)
    grad_down = (lax.dot_general(hidden, cotangent, (((0,), (0,)), ((), ())), preferred_element_type=jnp.float32) * keep_down).astype(jnp.bfloat16)
    grad_gate = (lax.dot_general(tokens, dgate, (((0,), (0,)), ((), ())), preferred_element_type=jnp.float32) * keep_gate).astype(jnp.bfloat16)
    grad_up = (lax.dot_general(tokens, dup, (((0,), (0,)), ((), ())), preferred_element_type=jnp.float32) * keep_up).astype(jnp.bfloat16)
    first = lax.dot_general(dgate, w_gate, (((1,), (1,)), ((), ())), preferred_element_type=jnp.float32)
    second = lax.dot_general(dup, w_up, (((1,), (1,)), ((), ())), preferred_element_type=jnp.float32)
    grad_input = (first + second).astype(jnp.bfloat16)
    return output, grad_input, grad_gate, grad_up, grad_down
```

```python
import jax
import jax.numpy as jnp
from jax import lax
from jax.sharding import PartitionSpec as P

BLOCK = 64


def expand(mask):
    return jnp.repeat(jnp.repeat(mask, BLOCK, 0), BLOCK, 1).astype(jnp.bfloat16)


def contract_last(left, right):
    return lax.dot_general(
        left, right, (((1,), (1,)), ((), ())), preferred_element_type=jnp.float32
    )


def contract_first(left, right):
    return lax.dot_general(
        left, right, (((0,), (0,)), ((), ())), preferred_element_type=jnp.float32
    )


def backward_gates(dhid, gate, up):
    sigma = jax.nn.sigmoid(gate)
    dgate = (dhid * up * sigma * (1.0 + gate * (1.0 - sigma))).astype(jnp.bfloat16)
    dup = (dhid * gate * sigma).astype(jnp.bfloat16)
    return (dgate, dup)


def body(tokens, gate_weight, up_weight, down_weight, mask_gate, mask_up, mask_down, cotangent):
    keep_gate = expand(mask_gate)
    keep_up = expand(mask_up)
    keep_down = expand(mask_down)
    w_gate = gate_weight * keep_gate
    w_up = up_weight * keep_up
    w_down = down_weight * keep_down
    width = w_gate.shape[1]
    pair = lax.all_gather(
        jnp.concatenate([tokens, cotangent], axis=1), "col", axis=0, tiled=True
    )
    depth = tokens.shape[1]
    panel = pair[:, :depth]
    cot_panel = pair[:, depth:]
    parts = jnp.concatenate(
        [
            jnp.dot(panel, w_gate, preferred_element_type=jnp.float32).astype(jnp.bfloat16),
            jnp.dot(panel, w_up, preferred_element_type=jnp.float32).astype(jnp.bfloat16),
            contract_last(cot_panel, w_down).astype(jnp.bfloat16),
        ],
        axis=1,
    )
    rows = parts.shape[0] // 4
    swapped = lax.all_to_all(parts, "row", 0, 0, tiled=True)
    total = jnp.sum(swapped.reshape(4, rows, 3 * width).astype(jnp.float32), axis=0)
    gate = total[:, :width]
    up = total[:, width : 2 * width]
    dhid = total[:, 2 * width :]
    hidden = (jax.nn.silu(gate) * up).astype(jnp.bfloat16)
    dgate, dup = backward_gates(dhid, gate, up)
    whole = lax.all_gather(
        jnp.concatenate([hidden, dgate, dup], axis=1), "row", axis=0, tiled=True
    )
    hidden = whole[:, :width]
    dgate = whole[:, width : 2 * width]
    dup = whole[:, 2 * width :]
    both = jnp.concatenate(
        [
            jnp.dot(hidden, w_down, preferred_element_type=jnp.float32).astype(jnp.bfloat16),
            (contract_last(dgate, w_gate) + contract_last(dup, w_up)).astype(jnp.bfloat16),
        ],
        axis=1,
    )
    spread = lax.all_to_all(both, "col", 0, 0, tiled=True)
    grad_down = (contract_first(hidden, cot_panel) * keep_down).astype(jnp.bfloat16)
    grad_gate = (contract_first(panel, dgate) * keep_gate).astype(jnp.bfloat16)
    grad_up = (contract_first(panel, dup) * keep_up).astype(jnp.bfloat16)
    spread = spread.reshape(-1, tokens.shape[0], 2 * depth).astype(jnp.float32)
    owned = jnp.sum(spread, axis=0).astype(jnp.bfloat16)
    output = owned[:, :depth]
    grad_input = owned[:, depth:]
    return (output, grad_input, grad_gate, grad_up, grad_down)


def solution(mesh):
    return jax.shard_map(
        body,
        mesh=mesh,
        in_specs=(
            P("col", "row"),
            P("row", "col"),
            P("row", "col"),
            P("col", "row"),
            P("row", "col"),
            P("row", "col"),
            P("col", "row"),
            P("col", "row"),
        ),
        out_specs=(
            P("col", "row"),
            P("col", "row"),
            P("row", "col"),
            P("row", "col"),
            P("col", "row"),
        ),
        check_vma=False,
    )
```
